32 devices in a mesh: group: 2 (over x), src: 8 (over z, y), tile: 2 (over core).
Axes of the slice: x: 2, y: 2, z: 4, core: 2. Of those that a mesh axis runs over, the one named last changes fastest.
Arguments:
- near_field: bfloat16 [4, 64, 2, 3, 512], P(('group', 'tile'), 'src'), parts along dimension 0, may hold values from -6 to 6
- x_taps: bfloat16 [8, 2, 8, 65], P('src'), may hold values from -0.5 to 0.5
- y_taps: bfloat16 [8, 2, 8, 65], P('src'), may hold values from -0.1875 to 0.1875
- source_weight: float32 [8], P('src'), may hold values from 0.0125 to 0.125
Outputs:
- intensity: float32 [4, 64, 512], P(('group', 'tile'), 'src'), parts along dimension 0
The draws below stay inside these ranges and needn't reach their ends.
There are 2 independent parts, one for each index of `group`. The reference program is written for one: setup_inputs(seed, part) draws one part's arguments, and reference() takes and returns one part's arrays. A program takes and returns all parts, laid end to end along the dimension named above; an argument that names none is the same for every part. Nothing has to cross between parts.
All inputs are finite; a program needn't handle non-finite values.
Results may differ from the reference program's by a relative error of at most 0.00054.
Values may be sent and summed in bfloat16 or wider, within the bound.
A program may use at most 128 MiB of HBM per device.

```python
import math
import jax
import jax.numpy as jnp
from jax import lax

COMPS = 3
RANK = 8
TAPS = 65
W = 512
TR = 64
SOURCES = 8
N_TILE = 2


def steps_of(key, shape, cuts, least, largest):
    def one(dim, blocks):
        steps = jax.random.uniform(jax.random.fold_in(jax.random.fold_in(key, 6), dim), (blocks,), jnp.float32, least / len(cuts), largest / len(cuts))
        return jnp.repeat(jnp.exp(steps), shape[dim] // blocks).reshape((-1,) + (1,) * (len(shape) - dim - 1))

    gain = one(*cuts[0])
    for cut in cuts[1:]:
        gain = gain * one(*cut)
    return gain


def centred(rng, extent, scale, reach, split=(), held_as=jnp.bfloat16):
    values = jax.random.normal(rng, extent, jnp.float32) * scale
    if len(split) > 0:
        values = steps_of(rng, extent, split, -0.22, 0.18) * values
    return jnp.clip(values, min=-reach, max=reach).astype(held_as)


def setup_inputs(seed: int = 0, part: int = 0) -> dict:
    seeds = jax.random.split(jax.random.key(seed), 5)
    part_splits = jax.random.split(jax.random.fold_in(seeds[4], part), 5)
    return {
        "near_field": centred(part_splits[0], (N_TILE, TR, 2, COMPS, W), 1.0, 6.0, ((0, 2), (1, 8))),
        "x_taps": centred(seeds[1], (SOURCES, 2, RANK, TAPS), (2 * TAPS) ** -0.5, 0.5, ((0, 8),)),
        "y_taps": centred(seeds[2], (SOURCES, 2, RANK, TAPS), (2 * RANK * TAPS) ** -0.5, 0.1875, ((0, 8),)),
        "source_weight": jnp.clip(jnp.exp(math.log(0.125) - 2.3025851 * jax.random.uniform(seeds[3], (SOURCES,), jnp.float32) ** steps_of(seeds[3], (SOURCES,), ((0, 8),), -0.2, 0.2)), 0.0125, 0.125),
    }


def reference(near_field, x_taps, y_taps, source_weight):
    tiles, tile_rows, _, comps, width = near_field.shape
    slab_rows = tiles * tile_rows
    ranks = x_taps.shape[2]
    rim_width = (x_taps.shape[-1] - 1) // 2
    field = near_field.astype(jnp.float32).reshape(slab_rows, 2, comps, width)
    lhs_columns = field.transpose(0, 2, 1, 3).reshape(slab_rows * comps, 2, width)

    def one_source(total, inputs):
        column_taps, row_taps, weight = inputs
        column_f = column_taps.astype(jnp.float32)
        col_re, col_im = column_f[0], column_f[1]
        kernel_x = jnp.stack([jnp.stack([col_re, -col_im], axis=1), jnp.stack([col_im, col_re], axis=1)], axis=0)
        kernel_x = kernel_x.reshape(2 * ranks, 2, -1)
        passed = lax.conv_general_dilated(lhs_columns, kernel_x, (1,), [(rim_width, rim_width)],
                                          dimension_numbers=("NCH", "OIH", "NCH"),
                                          precision=lax.Precision.HIGHEST)
        passed = lax.optimization_barrier(passed.astype(jnp.bfloat16)).astype(jnp.float32)
        passed = passed.reshape(slab_rows, comps, 2, ranks, width)
        lhs_rows = passed.transpose(1, 4, 2, 3, 0).reshape(comps * width, 2 * ranks, slab_rows)
        row_f = row_taps.astype(jnp.float32)
        row_re, row_im = row_f[0], row_f[1]
        kernel_y = jnp.stack([jnp.stack([row_re, -row_im], axis=0), jnp.stack([row_im, row_re], axis=0)], axis=0)
        kernel_y = kernel_y.reshape(2, 2 * ranks, -1)
        image = lax.conv_general_dilated(lhs_rows, kernel_y, (1,), [(rim_width, rim_width)],
                                         dimension_numbers=("NCH", "OIH", "NCH"),
                                         precision=lax.Precision.HIGHEST)
        power = jnp.sum((image * image).reshape(comps, width, 2, slab_rows), axis=(0, 2))
        return total + weight * power.T, None

    start_total = jnp.zeros((slab_rows, width), jnp.float32)
    total, _ = lax.scan(one_source, start_total, (x_taps, y_taps, source_weight))
    return total.reshape(tiles, tile_rows, width)
```

```python
import functools

import jax
import jax.numpy as jnp
from jax import lax
from jax.experimental import pallas as pl
from jax.experimental.pallas import tpu as pltpu
from jax.sharding import PartitionSpec as P

MESH = pl.DeviceIdType.MESH
BLOCK = 64
WINDOW = 128
NT = (((1,), (1,)), ((), ()))


def toeplitz(row):
    spread = jnp.broadcast_to(row, (BLOCK, WINDOW))
    return pltpu.roll(spread, 0, 1, stride=1, stride_axis=0)


def kernel(dims, field_ref, taps_ref, out_ref, window, taps_all, field32, fields,
           col_mat, row_mat, passed, acc, mine, gathered,
           f_send, f_recv, f_self, t_send, t_recv, t_self, o_send, o_recv):
    n_src, n_tile, local_rows, comps, ranks, tap_count = dims
    slots = WINDOW // local_rows
    per_group = BLOCK // local_rows
    halo = (WINDOW - BLOCK) // 2 // local_rows
    col_blocks = field_ref.shape[0]
    groups = n_src // per_group
    me = lax.axis_index("src")
    tile = lax.axis_index("tile")
    flat = tile * n_src + me
    devices = n_src * n_tile

    barrier = pltpu.get_barrier_semaphore()

    def greet(step, carry):
        other = lax.rem(flat + step, devices)
        pl.semaphore_signal(
            barrier, inc=1, device_id={"src": lax.rem(other, n_src), "tile": other // n_src},
            device_id_type=MESH)
        return carry

    lax.fori_loop(1, devices, greet, 0)
    pl.semaphore_wait(barrier, devices - 1)

    own_group = flat // per_group
    place = lax.rem(flat, per_group)
    upper = place >= per_group - halo
    second = jnp.where(upper, own_group + 1, own_group - 1)
    second_ok = jnp.logical_and(second >= 0, second < groups * n_tile)
    my_col = lax.rem(me, col_blocks)
    my_row = me // col_blocks

    def field_copy(col, row_group, slot, sem):
        to_tile = row_group // groups
        to_src = lax.rem(row_group, groups) * col_blocks + col
        return pltpu.make_async_remote_copy(
            src_ref=field_ref.at[col], dst_ref=window.at[slot],
            send_sem=f_send.at[sem], recv_sem=f_recv.at[slot],
            device_id={"src": to_src, "tile": to_tile}, device_id_type=MESH)

    first_slot = place + halo
    second_slot = jnp.where(upper, place + halo - per_group, place + halo + per_group)
    self_copy = pltpu.make_async_copy(field_ref.at[my_col], window.at[first_slot], f_self)
    self_taps = pltpu.make_async_copy(taps_ref, taps_all.at[me], t_self)

    def is_self(col):
        return own_group * col_blocks + col == flat

    def taps_copy(step):
        return pltpu.make_async_remote_copy(
            src_ref=taps_ref, dst_ref=taps_all.at[me],
            send_sem=t_send.at[step], recv_sem=t_recv.at[me],
            device_id={"src": lax.rem(me + step, n_src)}, device_id_type=MESH)

    self_copy.start()
    self_taps.start()

    def send_fields(step, carry):
        col = lax.rem(my_col + step, col_blocks)

        @pl.when(jnp.logical_not(is_self(col)))
        def _():
            field_copy(col, own_group, first_slot, step).start()

        @pl.when(second_ok)
        def _():
            field_copy(col, second, second_slot, col_blocks + step).start()

        return carry

    lax.fori_loop(0, col_blocks, send_fields, 0)

    def send_taps(step, carry):
        taps_copy(step).start()
        return carry

    lax.fori_loop(1, n_src, send_taps, 0)

    first_block = (tile * groups + my_row) * per_group - halo
    self_copy.wait()
    for slot in range(slots):
        block = first_block + slot
        ok = jnp.logical_and(block >= 0, block < devices)

        @pl.when(jnp.logical_and(ok, block != flat))
        def _():
            pltpu.make_async_remote_copy(
                src_ref=window.at[slot], dst_ref=window.at[slot],
                send_sem=f_send.at[0], recv_sem=f_recv.at[slot],
                device_id={"src": me}, device_id_type=MESH).wait_recv()

        rows = pl.ds(slot * local_rows, local_rows)

        @pl.when(ok)
        def _():
            got = window[slot].astype(jnp.float32)
            for part in range(2 * comps):
                field32[part, rows, :] = got[part * local_rows:(part + 1) * local_rows]

        @pl.when(jnp.logical_not(ok))
        def _():
            for part in range(2 * comps):
                field32[part, rows, :] = jnp.zeros((local_rows, WINDOW), jnp.float32)

    for comp in range(comps):
        real = field32[2 * comp]
        imag = field32[2 * comp + 1]
        top = pl.ds(comp * WINDOW, WINDOW)
        low = pl.ds((comps + comp) * WINDOW, WINDOW)
        fields[top, :WINDOW] = real.astype(jnp.bfloat16)
        fields[top, WINDOW:] = (-imag).astype(jnp.bfloat16)
        fields[low, :WINDOW] = imag.astype(jnp.bfloat16)
        fields[low, WINDOW:] = real.astype(jnp.bfloat16)

    self_taps.wait()

    def wait_taps(step, carry):
        source = lax.rem(me + step, n_src)
        pltpu.make_async_remote_copy(
            src_ref=taps_ref, dst_ref=taps_all.at[source],
            send_sem=t_send.at[step], recv_sem=t_recv.at[source],
            device_id={"src": source}, device_id_type=MESH).wait_recv()
        return carry

    lax.fori_loop(1, n_src, wait_taps, 0)

    acc[...] = jnp.zeros_like(acc)
    lane = lax.broadcasted_iota(jnp.int32, (4 * ranks, WINDOW), 1)

    def one_source(source, carry):
        raw = taps_all[source].astype(jnp.float32)
        taps = jnp.where(lane < tap_count, raw, 0.0)
        weight = jnp.sum(
            jnp.where(lane[0:1] >= WINDOW - 3, raw[0:1], 0.0), axis=1, keepdims=True)
        for rank in range(ranks):
            across = pl.ds(rank * BLOCK, BLOCK)
            for part in range(2):
                index = part * ranks + rank
                col_mat[across, part * WINDOW:(part + 1) * WINDOW] = toeplitz(
                    taps[index:index + 1]).astype(jnp.bfloat16)
            real = toeplitz(taps[2 * ranks + rank:2 * ranks + rank + 1])
            imag = toeplitz(taps[3 * ranks + rank:3 * ranks + rank + 1])
            base = 2 * rank * WINDOW
            row_mat[:BLOCK, base:base + WINDOW] = real.astype(jnp.bfloat16)
            row_mat[:BLOCK, base + WINDOW:base + 2 * WINDOW] = (-imag).astype(jnp.bfloat16)
            row_mat[BLOCK:, base:base + WINDOW] = imag.astype(jnp.bfloat16)
            row_mat[BLOCK:, base + WINDOW:base + 2 * WINDOW] = real.astype(jnp.bfloat16)
        for pair in range(comps):
            some = lax.dot_general(
                col_mat[...], fields[2 * pair * WINDOW:2 * (pair + 1) * WINDOW, :], NT,
                preferred_element_type=jnp.float32).astype(jnp.bfloat16)
            for half in range(2):
                part, comp = divmod(2 * pair + half, comps)
                for rank in range(ranks):
                    base = (2 * rank + part) * WINDOW
                    passed[comp * BLOCK:(comp + 1) * BLOCK, base:base + WINDOW] = some[
                        rank * BLOCK:(rank + 1) * BLOCK, half * WINDOW:(half + 1) * WINDOW]
        image = lax.dot_general(
            passed[...], row_mat[...], NT, preferred_element_type=jnp.float32)
        power = image * image
        total = power[:BLOCK]
        for comp in range(1, comps):
            total = total + power[comp * BLOCK:(comp + 1) * BLOCK]
        acc[:BLOCK, :] += weight * total
        return carry

    lax.fori_loop(0, n_src, one_source, 0)

    turned = acc[...].T
    block_image = turned[:BLOCK] + turned[BLOCK:]
    for owner in range(per_group):
        mine[owner] = block_image[owner * local_rows:(owner + 1) * local_rows]

    my_place = lax.rem(me, per_group)

    def out_copy(step):
        owner = lax.rem(my_place + step, per_group)
        return pltpu.make_async_remote_copy(
            src_ref=mine.at[owner], dst_ref=gathered.at[my_col],
            send_sem=o_send.at[step], recv_sem=o_recv.at[my_col],
            device_id={"src": my_row * per_group + owner}, device_id_type=MESH)

    def send_out(step, carry):
        out_copy(step).start()
        return carry

    lax.fori_loop(1, per_group, send_out, 0)
    gathered[my_col] = mine[my_place]

    def wait_out(step, carry):
        col = lax.rem(my_col + step, col_blocks)
        pltpu.make_async_remote_copy(
            src_ref=gathered.at[col], dst_ref=gathered.at[col],
            send_sem=o_send.at[0], recv_sem=o_recv.at[col],
            device_id={"src": me}, device_id_type=MESH).wait_recv()
        return carry

    lax.fori_loop(1, col_blocks, wait_out, 0)
    for pair in range(col_blocks // 2):
        out_ref[0, :, pair * WINDOW:(pair + 1) * WINDOW] = gathered[2 * pair] + pltpu.roll(
            gathered[2 * pair + 1], BLOCK, 1)

    def drain(step, carry):
        col = lax.rem(my_col + step, col_blocks)

        @pl.when(jnp.logical_not(is_self(col)))
        def _():
            field_copy(col, own_group, first_slot, step).wait_send()

        @pl.when(second_ok)
        def _():
            field_copy(col, second, second_slot, col_blocks + step).wait_send()

        return carry

    lax.fori_loop(0, col_blocks, drain, 0)

    def drain_taps(step, carry):
        taps_copy(step).wait_send()
        return carry

    lax.fori_loop(1, n_src, drain_taps, 0)

    def drain_out(step, carry):
        out_copy(step).wait_send()
        return carry

    lax.fori_loop(1, per_group, drain_out, 0)


def per_device(near_field, x_taps, y_taps, source_weight):
    n_src = lax.axis_size("src")
    n_tile = lax.axis_size("tile")
    _, local_rows, _, comps, width = near_field.shape
    _, _, ranks, tap_count = x_taps.shape
    rim = (tap_count - 1) // 2
    col_blocks = width // BLOCK
    per_group = BLOCK // local_rows
    assert WINDOW == BLOCK + 2 * rim and x_taps.shape[0] == 1
    assert n_src == col_blocks * (n_src * local_rows // BLOCK) and per_group == col_blocks

    rows_last = near_field[0].transpose(2, 1, 0, 3).reshape(2 * comps * local_rows, width)
    padded = jnp.pad(rows_last, ((0, 0), (rim, rim)))
    windows = jnp.stack([padded[:, BLOCK * k:BLOCK * k + WINDOW] for k in range(col_blocks)])

    high = lax.reduce_precision(source_weight, 8, 7)
    rest = source_weight - high
    middle = lax.reduce_precision(rest, 8, 7)
    low = rest - middle
    weights = jnp.broadcast_to(
        jnp.stack([high, middle, low], axis=1).astype(jnp.bfloat16), (4 * ranks, 3))
    taps = jnp.concatenate(
        [x_taps.reshape(2 * ranks, tap_count), y_taps.reshape(2 * ranks, tap_count)], axis=0)
    taps = jnp.concatenate([jnp.pad(taps, ((0, 0), (0, WINDOW - 3 - tap_count))), weights], axis=1)

    slots = WINDOW // local_rows
    dma = pltpu.SemaphoreType.DMA
    bf16, f32 = jnp.bfloat16, jnp.float32
    vmem = pl.BlockSpec(memory_space=pltpu.VMEM)
    dims = (n_src, n_tile, local_rows, comps, ranks, tap_count)
    return pl.pallas_call(
        functools.partial(kernel, dims),
        out_shape=jax.ShapeDtypeStruct((1, local_rows, width), f32),
        in_specs=[vmem, vmem],
        out_specs=vmem,
        scratch_shapes=[
            pltpu.VMEM((slots, 2 * comps * local_rows, WINDOW), bf16),
            pltpu.VMEM((n_src, 4 * ranks, WINDOW), bf16),
            pltpu.VMEM((2 * comps, WINDOW, WINDOW), f32),
            pltpu.VMEM((2 * comps * WINDOW, 2 * WINDOW), bf16),
            pltpu.VMEM((ranks * BLOCK, 2 * WINDOW), bf16),
            pltpu.VMEM((2 * BLOCK, 2 * ranks * WINDOW), bf16),
            pltpu.VMEM((comps * BLOCK, 2 * ranks * WINDOW), bf16),
            pltpu.VMEM((WINDOW, WINDOW), f32),
            pltpu.VMEM((per_group, local_rows, WINDOW), f32),
            pltpu.VMEM((col_blocks, local_rows, WINDOW), f32),
            dma((2 * col_blocks,)),
            dma((slots,)),
            dma,
            dma((n_src,)),
            dma((n_src,)),
            dma,
            dma((per_group,)),
            dma((col_blocks,)),
        ],
        compiler_params=pltpu.CompilerParams(collective_id=0, has_side_effects=True),
    )(windows, taps)


def solution(mesh):
    placed = (
        P(("group", "tile"), "src", None, None, None),
        P("src", None, None, None),
        P("src", None, None, None),
        P("src"),
    )
    return jax.shard_map(
        per_device,
        mesh=mesh,
        in_specs=placed,
        out_specs=P(("group", "tile"), "src", None),
        check_vma=False,
    )
```

```python
import functools

import jax
import jax.numpy as jnp
from jax import lax
from jax.experimental import pallas as pl
from jax.experimental.pallas import tpu as pltpu
from jax.sharding import PartitionSpec as P

MESH = pl.DeviceIdType.MESH
BLOCK = 64
WINDOW = 128
NT = (((1,), (1,)), ((), ()))


def toeplitz(row):
    spread = jnp.broadcast_to(row, (BLOCK, WINDOW))
    return pltpu.roll(spread, 0, 1, stride=1, stride_axis=0)


def kernel(dims, field_hbm, x_hbm, y_hbm, weight_hbm, out_ref, raw, x_raw, y_raw, weight,
           stage, field_ref, taps_ref, window, taps_all, field32, fields,
           col_mat, row_mat, passed, acc, mine, gathered,
           in_sem, f_send, f_recv, t_send, t_recv, o_send, o_recv):
    n_src, n_tile, local_rows, comps, ranks, tap_count = dims
    rim = (WINDOW - BLOCK) // 2
    width = raw.shape[-1]
    loads = [
        pltpu.make_async_copy(x_hbm, x_raw, in_sem.at[0]),
        pltpu.make_async_copy(y_hbm, y_raw, in_sem.at[1]),
        pltpu.make_async_copy(weight_hbm, weight, in_sem.at[2]),
        pltpu.make_async_copy(field_hbm, raw, in_sem.at[3]),
    ]
    for load in loads:
        load.start()
    slots = WINDOW // local_rows
    per_group = BLOCK // local_rows
    halo = (WINDOW - BLOCK) // 2 // local_rows
    col_blocks = field_ref.shape[0]
    groups = n_src // per_group
    me = lax.axis_index("src")
    tile = lax.axis_index("tile")
    flat = tile * n_src + me
    devices = n_src * n_tile

    barrier = pltpu.get_barrier_semaphore()

    def greet(step, carry):
        other = lax.rem(flat + step, devices)
        pl.semaphore_signal(
            barrier, inc=1, device_id={"src": lax.rem(other, n_src), "tile": other // n_src},
            device_id_type=MESH)
        return carry

    lax.fori_loop(1, devices, greet, 0)

    for load in loads[:3]:
        load.wait()
    whole = weight[...]
    high = whole.astype(jnp.bfloat16).astype(jnp.float32)
    middle = (whole - high).astype(jnp.bfloat16).astype(jnp.float32)
    low = whole - high - middle
    lane = lax.broadcasted_iota(jnp.int32, (4 * ranks, WINDOW), 1)
    spare = jnp.where(lane == WINDOW - 1, high, jnp.where(lane == WINDOW - 2, middle, low))
    taps32 = acc.at[:4 * ranks]
    taps32[...] = spare
    for part in range(2):
        taps32[part * ranks:(part + 1) * ranks, :tap_count] = x_raw[part].astype(jnp.float32)
        taps32[(2 + part) * ranks:(3 + part) * ranks, :tap_count] = y_raw[part].astype(
            jnp.float32)
    taps_ref[...] = taps32[...].astype(jnp.bfloat16)

    loads[3].wait()
    edge = jnp.zeros((stage.shape[0], WINDOW), jnp.float32)
    stage[:, :WINDOW] = edge
    stage[:, width:width + WINDOW] = edge
    for pair in range(raw.shape[0]):
        stage[2 * pair:2 * pair + 2, rim:rim + width] = raw[pair].astype(jnp.float32)
    for col in range(field_ref.shape[0]):
        field_ref[col] = stage[:, col * BLOCK:col * BLOCK + WINDOW].astype(jnp.bfloat16)

    own_group = flat // per_group
    place = lax.rem(flat, per_group)
    upper = place >= per_group - halo
    second = jnp.where(upper, own_group + 1, own_group - 1)
    second_ok = jnp.logical_and(second >= 0, second < groups * n_tile)
    my_col = lax.rem(me, col_blocks)
    my_row = me // col_blocks

    def field_copy(col, row_group, slot, sem):
        to_tile = row_group // groups
        to_src = lax.rem(row_group, groups) * col_blocks + col
        return pltpu.make_async_remote_copy(
            src_ref=field_ref.at[col], dst_ref=window.at[slot],
            send_sem=f_send.at[sem], recv_sem=f_recv.at[slot],
            device_id={"src": to_src, "tile": to_tile}, device_id_type=MESH)

    first_slot = place + halo
    second_slot = jnp.where(upper, place + halo - per_group, place + halo + per_group)

    def is_self(col):
        return own_group * col_blocks + col == flat

    def taps_copy(step):
        return pltpu.make_async_remote_copy(
            src_ref=taps_ref, dst_ref=taps_all.at[me],
            send_sem=t_send.at[step], recv_sem=t_recv.at[me],
            device_id={"src": lax.rem(me + step, n_src)}, device_id_type=MESH)

    pl.semaphore_wait(barrier, devices - 1)

    def send_fields(step, carry):
        col = lax.rem(my_col + step, col_blocks)

        @pl.when(jnp.logical_not(is_self(col)))
        def _():
            field_copy(col, own_group, first_slot, step).start()

        @pl.when(second_ok)
        def _():
            field_copy(col, second, second_slot, col_blocks + step).start()

        return carry

    def send_taps(step, carry):
        taps_copy(step).start()
        return carry

    lax.fori_loop(1, n_src, send_taps, 0)
    lax.fori_loop(0, col_blocks, send_fields, 0)

    first_block = (tile * groups + my_row) * per_group - halo
    window[first_slot] = field_ref[my_col]
    taps_all[me] = taps_ref[...]
    for slot in range(slots):
        block = first_block + slot
        ok = jnp.logical_and(block >= 0, block < devices)

        @pl.when(jnp.logical_not(ok))
        def _():
            window[slot] = jnp.zeros(window.shape[1:], window.dtype)

        @pl.when(jnp.logical_and(ok, block != flat))
        def _():
            pltpu.make_async_remote_copy(
                src_ref=window.at[slot], dst_ref=window.at[slot],
                send_sem=f_send.at[0], recv_sem=f_recv.at[slot],
                device_id={"src": me}, device_id_type=MESH).wait_recv()

    rows = local_rows * 2 * comps
    for slot in range(slots):
        field32[slot * rows:(slot + 1) * rows, :] = window[slot].astype(jnp.float32)
    for comp in range(comps):
        real = field32[pl.ds(2 * comp, WINDOW, stride=2 * comps), :]
        imag = field32[pl.ds(2 * comp + 1, WINDOW, stride=2 * comps), :]
        top = pl.ds(comp * WINDOW, WINDOW)
        low = pl.ds((comps + comp) * WINDOW, WINDOW)
        fields[top, :WINDOW] = real.astype(jnp.bfloat16)
        fields[top, WINDOW:] = (-imag).astype(jnp.bfloat16)
        fields[low, :WINDOW] = imag.astype(jnp.bfloat16)
        fields[low, WINDOW:] = real.astype(jnp.bfloat16)

    def wait_taps(step, carry):
        source = lax.rem(me + step, n_src)
        pltpu.make_async_remote_copy(
            src_ref=taps_ref, dst_ref=taps_all.at[source],
            send_sem=t_send.at[step], recv_sem=t_recv.at[source],
            device_id={"src": source}, device_id_type=MESH).wait_recv()
        return carry

    lax.fori_loop(1, n_src, wait_taps, 0)

    acc[...] = jnp.zeros_like(acc)

    def one_source(source, carry):
        raw = taps_all[source].astype(jnp.float32)
        taps = jnp.where(lane < tap_count, raw, 0.0)
        weight = jnp.sum(
            jnp.where(lane[0:1] >= WINDOW - 3, raw[0:1], 0.0), axis=1, keepdims=True)
        for rank in range(ranks):
            across = pl.ds(rank * BLOCK, BLOCK)
            for part in range(2):
                index = part * ranks + rank
                col_mat[across, part * WINDOW:(part + 1) * WINDOW] = toeplitz(
                    taps[index:index + 1]).astype(jnp.bfloat16)
            real = toeplitz(taps[2 * ranks + rank:2 * ranks + rank + 1])
            imag = toeplitz(taps[3 * ranks + rank:3 * ranks + rank + 1])
            base = 2 * rank * WINDOW
            row_mat[:BLOCK, base:base + WINDOW] = real.astype(jnp.bfloat16)
            row_mat[:BLOCK, base + WINDOW:base + 2 * WINDOW] = (-imag).astype(jnp.bfloat16)
            row_mat[BLOCK:, base:base + WINDOW] = imag.astype(jnp.bfloat16)
            row_mat[BLOCK:, base + WINDOW:base + 2 * WINDOW] = real.astype(jnp.bfloat16)
        for pair in range(comps):
            some = lax.dot_general(
                col_mat[...], fields[2 * pair * WINDOW:2 * (pair + 1) * WINDOW, :], NT,
                preferred_element_type=jnp.float32).astype(jnp.bfloat16)
            for half in range(2):
                part, comp = divmod(2 * pair + half, comps)
                for rank in range(ranks):
                    base = (2 * rank + part) * WINDOW
                    passed[comp * BLOCK:(comp + 1) * BLOCK, base:base + WINDOW] = some[
                        rank * BLOCK:(rank + 1) * BLOCK, half * WINDOW:(half + 1) * WINDOW]
        image = lax.dot_general(
            passed[...], row_mat[...], NT, preferred_element_type=jnp.float32)
        power = image * image
        total = power[:BLOCK]
        for comp in range(1, comps):
            total = total + power[comp * BLOCK:(comp + 1) * BLOCK]
        acc[:BLOCK, :] += weight * total
        return carry

    lax.fori_loop(0, n_src, one_source, 0)

    turned = acc[...].T
    block_image = turned[:BLOCK] + turned[BLOCK:]
    for owner in range(per_group):
        mine[owner] = block_image[owner * local_rows:(owner + 1) * local_rows]

    my_place = lax.rem(me, per_group)

    def out_copy(step):
        owner = lax.rem(my_place + step, per_group)
        return pltpu.make_async_remote_copy(
            src_ref=mine.at[owner], dst_ref=gathered.at[my_col],
            send_sem=o_send.at[step], recv_sem=o_recv.at[my_col],
            device_id={"src": my_row * per_group + owner}, device_id_type=MESH)

    def send_out(step, carry):
        out_copy(step).start()
        return carry

    lax.fori_loop(1, per_group, send_out, 0)
    gathered[my_col] = mine[my_place]

    def wait_out(step, carry):
        col = lax.rem(my_col + step, col_blocks)
        pltpu.make_async_remote_copy(
            src_ref=gathered.at[col], dst_ref=gathered.at[col],
            send_sem=o_send.at[0], recv_sem=o_recv.at[col],
            device_id={"src": me}, device_id_type=MESH).wait_recv()
        return carry

    lax.fori_loop(1, col_blocks, wait_out, 0)
    for pair in range(col_blocks // 2):
        out_ref[0, :, pair * WINDOW:(pair + 1) * WINDOW] = gathered[2 * pair] + pltpu.roll(
            gathered[2 * pair + 1], BLOCK, 1)

    def drain(step, carry):
        col = lax.rem(my_col + step, col_blocks)

        @pl.when(jnp.logical_not(is_self(col)))
        def _():
            field_copy(col, own_group, first_slot, step).wait_send()

        @pl.when(second_ok)
        def _():
            field_copy(col, second, second_slot, col_blocks + step).wait_send()

        return carry

    lax.fori_loop(0, col_blocks, drain, 0)

    def drain_taps(step, carry):
        taps_copy(step).wait_send()
        return carry

    lax.fori_loop(1, n_src, drain_taps, 0)

    def drain_out(step, carry):
        out_copy(step).wait_send()
        return carry

    lax.fori_loop(1, per_group, drain_out, 0)


def per_device(near_field, x_taps, y_taps, source_weight):
    n_src = lax.axis_size("src")
    n_tile = lax.axis_size("tile")
    _, local_rows, _, comps, width = near_field.shape
    _, _, ranks, tap_count = x_taps.shape
    rim = (tap_count - 1) // 2
    col_blocks = width // BLOCK
    per_group = BLOCK // local_rows
    assert WINDOW == BLOCK + 2 * rim and x_taps.shape[0] == 1
    assert n_src == col_blocks * (n_src * local_rows // BLOCK) and per_group == col_blocks

    rows_last = near_field[0].transpose(0, 2, 1, 3).reshape(comps * local_rows, 2, width)
    slots = WINDOW // local_rows
    dma = pltpu.SemaphoreType.DMA
    bf16, f32 = jnp.bfloat16, jnp.float32
    vmem = pl.BlockSpec(memory_space=pltpu.VMEM)
    anywhere = pl.BlockSpec(memory_space=pl.ANY)
    dims = (n_src, n_tile, local_rows, comps, ranks, tap_count)
    return pl.pallas_call(
        functools.partial(kernel, dims),
        out_shape=jax.ShapeDtypeStruct((1, local_rows, width), f32),
        in_specs=[anywhere] * 4,
        out_specs=vmem,
        scratch_shapes=[
            pltpu.VMEM((comps * local_rows, 2, width), bf16),
            pltpu.VMEM((2, ranks, tap_count), bf16),
            pltpu.VMEM((2, ranks, tap_count), bf16),
            pltpu.VMEM((1, 1), f32),
            pltpu.VMEM((2 * comps * local_rows, width + WINDOW), f32),
            pltpu.VMEM((col_blocks, 2 * comps * local_rows, WINDOW), bf16),
            pltpu.VMEM((4 * ranks, WINDOW), bf16),
            pltpu.VMEM((slots, 2 * comps * local_rows, WINDOW), bf16),
            pltpu.VMEM((n_src, 4 * ranks, WINDOW), bf16),
            pltpu.VMEM((2 * comps * WINDOW, WINDOW), f32),
            pltpu.VMEM((2 * comps * WINDOW, 2 * WINDOW), bf16),
            pltpu.VMEM((ranks * BLOCK, 2 * WINDOW), bf16),
            pltpu.VMEM((2 * BLOCK, 2 * ranks * WINDOW), bf16),
            pltpu.VMEM((comps * BLOCK, 2 * ranks * WINDOW), bf16),
            pltpu.VMEM((WINDOW, WINDOW), f32),
            pltpu.VMEM((per_group, local_rows, WINDOW), f32),
            pltpu.VMEM((col_blocks, local_rows, WINDOW), f32),
            dma((4,)),
            dma((2 * col_blocks,)),
            dma((slots,)),
            dma((n_src,)),
            dma((n_src,)),
            dma((per_group,)),
            dma((col_blocks,)),
        ],
        compiler_params=pltpu.CompilerParams(collective_id=0, has_side_effects=True),
    )(rows_last, x_taps[0], y_taps[0], source_weight.reshape(1, 1))


def solution(mesh):
    placed = (
        P(("group", "tile"), "src", None, None, None),
        P("src", None, None, None),
        P("src", None, None, None),
        P("src"),
    )
    return jax.shard_map(
        per_device,
        mesh=mesh,
        in_specs=placed,
        out_specs=P(("group", "tile"), "src", None),
        check_vma=False,
    )
```

```python
import functools

import jax
import jax.numpy as jnp
from jax import lax
from jax.experimental import pallas as pl
from jax.experimental.pallas import tpu as pltpu
from jax.sharding import PartitionSpec as P

MESH = pl.DeviceIdType.MESH
BLOCK = 64
WINDOW = 128
NT = (((1,), (1,)), ((), ()))
HEAD = 1
TURNS = 7


def toeplitz(row):
    spread = jnp.broadcast_to(row, (BLOCK, WINDOW))
    return pltpu.roll(spread, 0, 1, stride=1, stride_axis=0)


def kernel(dims, field_hbm, x_hbm, y_hbm, weight_hbm, out_ref, raw, x_raw, y_raw, weight,
           stage, field_ref, taps_ref, window, taps_all, field32, fields,
           col_mat, row_mat, passed, acc, mine, gathered,
           in_sem, f_send, f_recv, t_send, t_recv, o_send, o_recv):
    n_src, n_tile, local_rows, comps, ranks, tap_count = dims
    rim = (WINDOW - BLOCK) // 2
    width = raw.shape[-1]
    loads = [
        pltpu.make_async_copy(x_hbm, x_raw, in_sem.at[0]),
        pltpu.make_async_copy(y_hbm, y_raw, in_sem.at[1]),
        pltpu.make_async_copy(weight_hbm, weight, in_sem.at[2]),
        pltpu.make_async_copy(field_hbm, raw, in_sem.at[3]),
    ]
    for load in loads:
        load.start()
    slots = WINDOW // local_rows
    per_group = BLOCK // local_rows
    halo = (WINDOW - BLOCK) // 2 // local_rows
    col_blocks = field_ref.shape[0]
    groups = n_src // per_group
    me = lax.axis_index("src")
    tile = lax.axis_index("tile")
    flat = tile * n_src + me
    devices = n_src * n_tile

    barrier = pltpu.get_barrier_semaphore()

    def greet(step, carry):
        other = lax.rem(flat + step, devices)
        pl.semaphore_signal(
            barrier, inc=1, device_id={"src": lax.rem(other, n_src), "tile": other // n_src},
            device_id_type=MESH)
        return carry

    lax.fori_loop(1, devices, greet, 0)

    for load in loads[:3]:
        load.wait()
    whole = weight[...]
    high = whole.astype(jnp.bfloat16).astype(jnp.float32)
    middle = (whole - high).astype(jnp.bfloat16).astype(jnp.float32)
    low = whole - high - middle
    lane = lax.broadcasted_iota(jnp.int32, (4 * ranks, WINDOW), 1)
    spare = jnp.where(lane == WINDOW - 1, high, jnp.where(lane == WINDOW - 2, middle, low))
    taps32 = acc.at[:4 * ranks]
    taps32[...] = spare
    for part in range(2):
        taps32[part * ranks:(part + 1) * ranks, :tap_count] = x_raw[part].astype(jnp.float32)
        taps32[(2 + part) * ranks:(3 + part) * ranks, :tap_count] = y_raw[part].astype(
            jnp.float32)
    taps_ref[...] = taps32[...].astype(jnp.bfloat16)

    loads[3].wait()
    edge = jnp.zeros((stage.shape[0], WINDOW), jnp.float32)
    stage[:, :WINDOW] = edge
    stage[:, width:width + WINDOW] = edge
    for pair in range(raw.shape[0]):
        stage[2 * pair:2 * pair + 2, rim:rim + width] = raw[pair].astype(jnp.float32)
    for col in range(field_ref.shape[0]):
        field_ref[col] = stage[:, col * BLOCK:col * BLOCK + WINDOW].astype(jnp.bfloat16)

    own_group = flat // per_group
    place = lax.rem(flat, per_group)
    upper = place >= per_group - halo
    second = jnp.where(upper, own_group + 1, own_group - 1)
    second_ok = jnp.logical_and(second >= 0, second < groups * n_tile)
    my_col = lax.rem(me, col_blocks)
    my_row = me // col_blocks

    def field_copy(col, row_group, slot, sem):
        to_tile = row_group // groups
        to_src = lax.rem(row_group, groups) * col_blocks + col
        return pltpu.make_async_remote_copy(
            src_ref=field_ref.at[col], dst_ref=window.at[slot],
            send_sem=f_send.at[sem], recv_sem=f_recv.at[slot],
            device_id={"src": to_src, "tile": to_tile}, device_id_type=MESH)

    first_slot = place + halo
    second_slot = jnp.where(upper, place + halo - per_group, place + halo + per_group)

    def is_self(col):
        return own_group * col_blocks + col == flat

    def taps_copy(step):
        return pltpu.make_async_remote_copy(
            src_ref=taps_ref, dst_ref=taps_all.at[me],
            send_sem=t_send.at[step], recv_sem=t_recv.at[me],
            device_id={"src": lax.rem(me + step, n_src)}, device_id_type=MESH)

    pl.semaphore_wait(barrier, devices - 1)

    def send_fields(step, carry):
        col = lax.rem(my_col + step, col_blocks)

        @pl.when(jnp.logical_not(is_self(col)))
        def _():
            field_copy(col, own_group, first_slot, step).start()

        @pl.when(second_ok)
        def _():
            field_copy(col, second, second_slot, col_blocks + step).start()

        return carry

    lax.fori_loop(0, col_blocks, send_fields, 0)

    def send_taps(step, carry):
        taps_copy(step).start()
        return carry

    lax.fori_loop(1, n_src, send_taps, 0)

    first_block = (tile * groups + my_row) * per_group - halo
    window[first_slot] = field_ref[my_col]
    taps_all[me] = taps_ref[...]
    for slot in range(slots):
        block = first_block + slot
        ok = jnp.logical_and(block >= 0, block < devices)

        @pl.when(jnp.logical_not(ok))
        def _():
            window[slot] = jnp.zeros(window.shape[1:], window.dtype)

        @pl.when(jnp.logical_and(ok, block != flat))
        def _():
            pltpu.make_async_remote_copy(
                src_ref=window.at[slot], dst_ref=window.at[slot],
                send_sem=f_send.at[0], recv_sem=f_recv.at[slot],
                device_id={"src": me}, device_id_type=MESH).wait_recv()

    rows = local_rows * 2 * comps
    for slot in range(slots):
        field32[slot * rows:(slot + 1) * rows, :] = window[slot].astype(jnp.float32)
    for comp in range(comps):
        real = field32[pl.ds(2 * comp, WINDOW, stride=2 * comps), :]
        imag = field32[pl.ds(2 * comp + 1, WINDOW, stride=2 * comps), :]
        top = pl.ds(comp * WINDOW, WINDOW)
        low = pl.ds((comps + comp) * WINDOW, WINDOW)
        fields[top, :WINDOW] = real.astype(jnp.bfloat16)
        fields[top, WINDOW:] = (-imag).astype(jnp.bfloat16)
        fields[low, :WINDOW] = imag.astype(jnp.bfloat16)
        fields[low, WINDOW:] = real.astype(jnp.bfloat16)

    def wait_taps(step, carry):
        source = lax.rem(me + step, n_src)
        pltpu.make_async_remote_copy(
            src_ref=taps_ref, dst_ref=taps_all.at[source],
            send_sem=t_send.at[step], recv_sem=t_recv.at[source],
            device_id={"src": source}, device_id_type=MESH).wait_recv()
        return carry


    acc[...] = jnp.zeros_like(acc)

    def one_source(source, slot):
        raw = taps_all[source].astype(jnp.float32)
        taps = jnp.where(lane < tap_count, raw, 0.0)
        weight = jnp.sum(
            jnp.where(lane[0:1] >= WINDOW - 3, raw[0:1], 0.0), axis=1, keepdims=True)
        for rank in range(ranks):
            across = pl.ds(rank * BLOCK, BLOCK)
            for part in range(2):
                index = part * ranks + rank
                col_mat[slot, across, part * WINDOW:(part + 1) * WINDOW] = toeplitz(
                    taps[index:index + 1]).astype(jnp.bfloat16)
            real = toeplitz(taps[2 * ranks + rank:2 * ranks + rank + 1])
            imag = toeplitz(taps[3 * ranks + rank:3 * ranks + rank + 1])
            base = 2 * rank * WINDOW
            row_mat[slot, :BLOCK, base:base + WINDOW] = real.astype(jnp.bfloat16)
            row_mat[slot, :BLOCK, base + WINDOW:base + 2 * WINDOW] = (-imag).astype(jnp.bfloat16)
            row_mat[slot, BLOCK:, base:base + WINDOW] = imag.astype(jnp.bfloat16)
            row_mat[slot, BLOCK:, base + WINDOW:base + 2 * WINDOW] = real.astype(jnp.bfloat16)
        for pair in range(comps):
            some = lax.dot_general(
                col_mat[slot], fields[2 * pair * WINDOW:2 * (pair + 1) * WINDOW, :], NT,
                preferred_element_type=jnp.float32).astype(jnp.bfloat16)
            for half in range(2):
                part, comp = divmod(2 * pair + half, comps)
                for rank in range(ranks):
                    base = (2 * rank + part) * WINDOW
                    passed[slot, comp * BLOCK:(comp + 1) * BLOCK, base:base + WINDOW] = some[
                        rank * BLOCK:(rank + 1) * BLOCK, half * WINDOW:(half + 1) * WINDOW]
        image = lax.dot_general(
            passed[slot], row_mat[slot], NT, preferred_element_type=jnp.float32)
        power = image * image
        total = power[:BLOCK]
        for comp in range(1, comps):
            total = total + power[comp * BLOCK:(comp + 1) * BLOCK]
        return weight * total

    def sources_from(first, count):
        total = None
        for turn in range(count):
            term = one_source(lax.rem(me + first + turn, n_src), turn)
            total = term if total is None else total + term
        acc[:BLOCK, :] += total

    def later_sources(step, carry):
        sources_from(HEAD + step * TURNS, TURNS)
        return carry

    lax.fori_loop(1, HEAD, wait_taps, 0)
    sources_from(0, HEAD)
    lax.fori_loop(HEAD, n_src, wait_taps, 0)
    rounds, rest = divmod(n_src - HEAD, TURNS)
    lax.fori_loop(0, rounds, later_sources, 0)
    if rest > 0:
        sources_from(HEAD + rounds * TURNS, rest)

    turned = acc[...].T
    block_image = turned[:BLOCK] + turned[BLOCK:]
    for owner in range(per_group):
        mine[owner] = block_image[owner * local_rows:(owner + 1) * local_rows]

    my_place = lax.rem(me, per_group)

    def out_copy(step):
        owner = lax.rem(my_place + step, per_group)
        return pltpu.make_async_remote_copy(
            src_ref=mine.at[owner], dst_ref=gathered.at[my_col],
            send_sem=o_send.at[step], recv_sem=o_recv.at[my_col],
            device_id={"src": my_row * per_group + owner}, device_id_type=MESH)

    def send_out(step, carry):
        out_copy(step).start()
        return carry

    lax.fori_loop(1, per_group, send_out, 0)
    gathered[my_col] = mine[my_place]

    def wait_out(step, carry):
        col = lax.rem(my_col + step, col_blocks)
        pltpu.make_async_remote_copy(
            src_ref=gathered.at[col], dst_ref=gathered.at[col],
            send_sem=o_send.at[0], recv_sem=o_recv.at[col],
            device_id={"src": me}, device_id_type=MESH).wait_recv()
        return carry

    lax.fori_loop(1, col_blocks, wait_out, 0)
    for pair in range(col_blocks // 2):
        out_ref[0, :, pair * WINDOW:(pair + 1) * WINDOW] = gathered[2 * pair] + pltpu.roll(
            gathered[2 * pair + 1], BLOCK, 1)

    def drain(step, carry):
        col = lax.rem(my_col + step, col_blocks)

        @pl.when(jnp.logical_not(is_self(col)))
        def _():
            field_copy(col, own_group, first_slot, step).wait_send()

        @pl.when(second_ok)
        def _():
            field_copy(col, second, second_slot, col_blocks + step).wait_send()

        return carry

    lax.fori_loop(0, col_blocks, drain, 0)

    def drain_taps(step, carry):
        taps_copy(step).wait_send()
        return carry

    lax.fori_loop(1, n_src, drain_taps, 0)

    def drain_out(step, carry):
        out_copy(step).wait_send()
        return carry

    lax.fori_loop(1, per_group, drain_out, 0)


def per_device(near_field, x_taps, y_taps, source_weight):
    n_src = lax.axis_size("src")
    n_tile = lax.axis_size("tile")
    _, local_rows, _, comps, width = near_field.shape
    _, _, ranks, tap_count = x_taps.shape
    rim = (tap_count - 1) // 2
    col_blocks = width // BLOCK
    per_group = BLOCK // local_rows
    assert WINDOW == BLOCK + 2 * rim and x_taps.shape[0] == 1
    assert n_src == col_blocks * (n_src * local_rows // BLOCK) and per_group == col_blocks

    rows_last = near_field[0].transpose(0, 2, 1, 3).reshape(comps * local_rows, 2, width)
    slots = WINDOW // local_rows
    dma = pltpu.SemaphoreType.DMA
    bf16, f32 = jnp.bfloat16, jnp.float32
    vmem = pl.BlockSpec(memory_space=pltpu.VMEM)
    anywhere = pl.BlockSpec(memory_space=pl.ANY)
    dims = (n_src, n_tile, local_rows, comps, ranks, tap_count)
    return pl.pallas_call(
        functools.partial(kernel, dims),
        out_shape=pltpu.VMEM((1, local_rows, width), f32),
        in_specs=[anywhere] * 4,
        out_specs=vmem,
        scratch_shapes=[
            pltpu.VMEM((comps * local_rows, 2, width), bf16),
            pltpu.VMEM((2, ranks, tap_count), bf16),
            pltpu.VMEM((2, ranks, tap_count), bf16),
            pltpu.VMEM((1, 1), f32),
            pltpu.VMEM((2 * comps * local_rows, width + WINDOW), f32),
            pltpu.VMEM((col_blocks, 2 * comps * local_rows, WINDOW), bf16),
            pltpu.VMEM((4 * ranks, WINDOW), bf16),
            pltpu.VMEM((slots, 2 * comps * local_rows, WINDOW), bf16),
            pltpu.VMEM((n_src, 4 * ranks, WINDOW), bf16),
            pltpu.VMEM((2 * comps * WINDOW, WINDOW), f32),
            pltpu.VMEM((2 * comps * WINDOW, 2 * WINDOW), bf16),
            pltpu.VMEM((TURNS, ranks * BLOCK, 2 * WINDOW), bf16),
            pltpu.VMEM((TURNS, 2 * BLOCK, 2 * ranks * WINDOW), bf16),
            pltpu.VMEM((TURNS, comps * BLOCK, 2 * ranks * WINDOW), bf16),
            pltpu.VMEM((WINDOW, WINDOW), f32),
            pltpu.VMEM((per_group, local_rows, WINDOW), f32),
            pltpu.VMEM((col_blocks, local_rows, WINDOW), f32),
            dma((4,)),
            dma((2 * col_blocks,)),
            dma((slots,)),
            dma((n_src,)),
            dma((n_src,)),
            dma((per_group,)),
            dma((col_blocks,)),
        ],
        compiler_params=pltpu.CompilerParams(collective_id=0, has_side_effects=True),
    )(rows_last, x_taps[0], y_taps[0], source_weight.reshape(1, 1))


def solution(mesh):
    placed = (
        P(("group", "tile"), "src", None, None, None),
        P("src", None, None, None),
        P("src", None, None, None),
        P("src"),
    )
    return jax.shard_map(
        per_device,
        mesh=mesh,
        in_specs=placed,
        out_specs=P(("group", "tile"), "src", None),
        check_vma=False,
    )
```

```python
import functools

import jax
import jax.numpy as jnp
from jax import lax
from jax.experimental import pallas as pl
from jax.experimental.pallas import tpu as pltpu
from jax.sharding import PartitionSpec as P

MESH = pl.DeviceIdType.MESH
BLOCK = 64
WINDOW = 128
NT = (((1,), (1,)), ((), ()))
HEAD = 1
TURNS = 7


def toeplitz(row):
    spread = jnp.broadcast_to(row, (BLOCK, WINDOW))
    return pltpu.roll(spread, 0, 1, stride=1, stride_axis=0)


def kernel(dims, field_hbm, x_hbm, y_hbm, weight_hbm, out_ref, raw, x_raw, y_raw, weight,
           stage, field_ref, taps_ref, window, taps_all, field32, fields,
           col_mat, row_mat, passed, acc, mine, gathered,
           in_sem, f_send, f_recv, t_send, t_recv, o_send, o_recv):
    n_src, n_tile, local_rows, comps, ranks, tap_count = dims
    rim = (WINDOW - BLOCK) // 2
    width = raw.shape[-1]
    loads = [
        pltpu.make_async_copy(x_hbm, x_raw, in_sem.at[0]),
        pltpu.make_async_copy(y_hbm, y_raw, in_sem.at[1]),
        pltpu.make_async_copy(weight_hbm, weight, in_sem.at[2]),
        pltpu.make_async_copy(field_hbm, raw, in_sem.at[3]),
    ]
    for load in loads:
        load.start()
    slots = WINDOW // local_rows
    per_group = BLOCK // local_rows
    halo = (WINDOW - BLOCK) // 2 // local_rows
    col_blocks = field_ref.shape[0]
    groups = n_src // per_group
    me = lax.axis_index("src")
    tile = lax.axis_index("tile")
    flat = tile * n_src + me
    devices = n_src * n_tile

    barrier = pltpu.get_barrier_semaphore()

    def greet(step, carry):
        other = lax.rem(flat + step, devices)
        pl.semaphore_signal(
            barrier, inc=1, device_id={"src": lax.rem(other, n_src), "tile": other // n_src},
            device_id_type=MESH)
        return carry

    lax.fori_loop(1, devices, greet, 0)

    for load in loads[:3]:
        load.wait()
    whole = weight[...]
    high = whole.astype(jnp.bfloat16).astype(jnp.float32)
    middle = (whole - high).astype(jnp.bfloat16).astype(jnp.float32)
    low = whole - high - middle
    lane = lax.broadcasted_iota(jnp.int32, (4 * ranks, WINDOW), 1)
    spare = jnp.where(lane == WINDOW - 1, high, jnp.where(lane == WINDOW - 2, middle, low))
    taps32 = acc.at[:4 * ranks]
    taps32[...] = spare
    for part in range(2):
        taps32[part * ranks:(part + 1) * ranks, :tap_count] = x_raw[part].astype(jnp.float32)
        taps32[(2 + part) * ranks:(3 + part) * ranks, :tap_count] = y_raw[part].astype(
            jnp.float32)
    taps_ref[...] = taps32[...].astype(jnp.bfloat16)

    loads[3].wait()
    edge = jnp.zeros((stage.shape[0], WINDOW), jnp.float32)
    stage[:, :WINDOW] = edge
    stage[:, width:width + WINDOW] = edge
    for pair in range(raw.shape[0]):
        stage[2 * pair:2 * pair + 2, rim:rim + width] = raw[pair].astype(jnp.float32)
    for col in range(field_ref.shape[0]):
        field_ref[col] = stage[:, col * BLOCK:col * BLOCK + WINDOW].astype(jnp.bfloat16)

    own_group = flat // per_group
    place = lax.rem(flat, per_group)
    upper = place >= per_group - halo
    second = jnp.where(upper, own_group + 1, own_group - 1)
    second_ok = jnp.logical_and(second >= 0, second < groups * n_tile)
    my_col = lax.rem(me, col_blocks)
    my_row = me // col_blocks

    def field_copy(col, row_group, slot, sem):
        to_tile = row_group // groups
        to_src = lax.rem(row_group, groups) * col_blocks + col
        return pltpu.make_async_remote_copy(
            src_ref=field_ref.at[col], dst_ref=window.at[slot],
            send_sem=f_send.at[sem], recv_sem=f_recv.at[slot],
            device_id={"src": to_src, "tile": to_tile}, device_id_type=MESH)

    first_slot = place + halo
    second_slot = jnp.where(upper, place + halo - per_group, place + halo + per_group)

    def is_self(col):
        return own_group * col_blocks + col == flat

    def taps_copy(step):
        return pltpu.make_async_remote_copy(
            src_ref=taps_ref, dst_ref=taps_all.at[me],
            send_sem=t_send.at[step], recv_sem=t_recv.at[me],
            device_id={"src": lax.rem(me + step, n_src)}, device_id_type=MESH)

    pl.semaphore_wait(barrier, devices - 1)

    def send_fields(step, carry):
        col = lax.rem(my_col + step, col_blocks)

        @pl.when(jnp.logical_not(is_self(col)))
        def _():
            field_copy(col, own_group, first_slot, step).start()

        @pl.when(second_ok)
        def _():
            field_copy(col, second, second_slot, col_blocks + step).start()

        return carry

    lax.fori_loop(0, col_blocks, send_fields, 0)

    def send_taps(step, carry):
        taps_copy(step).start()
        return carry

    lax.fori_loop(1, n_src, send_taps, 0)

    first_block = (tile * groups + my_row) * per_group - halo
    window[first_slot] = field_ref[my_col]
    taps_all[me] = taps_ref[...]
    for slot in range(slots):
        block = first_block + slot
        ok = jnp.logical_and(block >= 0, block < devices)

        @pl.when(jnp.logical_not(ok))
        def _():
            window[slot] = jnp.zeros(window.shape[1:], window.dtype)

        @pl.when(jnp.logical_and(ok, block != flat))
        def _():
            pltpu.make_async_remote_copy(
                src_ref=window.at[slot], dst_ref=window.at[slot],
                send_sem=f_send.at[0], recv_sem=f_recv.at[slot],
                device_id={"src": me}, device_id_type=MESH).wait_recv()

    rows = local_rows * 2 * comps
    for slot in range(slots):
        field32[slot * rows:(slot + 1) * rows, :] = window[slot].astype(jnp.float32)
    for comp in range(comps):
        real = field32[pl.ds(2 * comp, WINDOW, stride=2 * comps), :]
        imag = field32[pl.ds(2 * comp + 1, WINDOW, stride=2 * comps), :]
        top = pl.ds(comp * WINDOW, WINDOW)
        low = pl.ds((comps + comp) * WINDOW, WINDOW)
        fields[top, :WINDOW] = real.astype(jnp.bfloat16)
        fields[top, WINDOW:] = (-imag).astype(jnp.bfloat16)
        fields[low, :WINDOW] = imag.astype(jnp.bfloat16)
        fields[low, WINDOW:] = real.astype(jnp.bfloat16)

    def wait_taps(step, carry):
        source = lax.rem(me + step, n_src)
        pltpu.make_async_remote_copy(
            src_ref=taps_ref, dst_ref=taps_all.at[source],
            send_sem=t_send.at[step], recv_sem=t_recv.at[source],
            device_id={"src": source}, device_id_type=MESH).wait_recv()
        return carry


    acc[...] = jnp.zeros_like(acc)

    def column_pass(source, slot):
        raw = taps_all[source].astype(jnp.float32)
        taps = jnp.where(lane < tap_count, raw, 0.0)
        weight = jnp.sum(
            jnp.where(lane[0:1] >= WINDOW - 3, raw[0:1], 0.0), axis=1, keepdims=True)
        for rank in range(ranks):
            across = pl.ds(rank * BLOCK, BLOCK)
            for part in range(2):
                index = part * ranks + rank
                col_mat[slot, across, part * WINDOW:(part + 1) * WINDOW] = toeplitz(
                    taps[index:index + 1]).astype(jnp.bfloat16)
            real = toeplitz(taps[2 * ranks + rank:2 * ranks + rank + 1])
            imag = toeplitz(taps[3 * ranks + rank:3 * ranks + rank + 1])
            base = 2 * rank * WINDOW
            row_mat[slot, :BLOCK, base:base + WINDOW] = real.astype(jnp.bfloat16)
            row_mat[slot, :BLOCK, base + WINDOW:base + 2 * WINDOW] = (-imag).astype(jnp.bfloat16)
            row_mat[slot, BLOCK:, base:base + WINDOW] = imag.astype(jnp.bfloat16)
            row_mat[slot, BLOCK:, base + WINDOW:base + 2 * WINDOW] = real.astype(jnp.bfloat16)
        for pair in range(comps):
            some = lax.dot_general(
                col_mat[slot], fields[2 * pair * WINDOW:2 * (pair + 1) * WINDOW, :], NT,
                preferred_element_type=jnp.float32).astype(jnp.bfloat16)
            for half in range(2):
                part, comp = divmod(2 * pair + half, comps)
                for rank in range(ranks):
                    base = (2 * rank + part) * WINDOW
                    passed[slot, comp * BLOCK:(comp + 1) * BLOCK, base:base + WINDOW] = some[
                        rank * BLOCK:(rank + 1) * BLOCK, half * WINDOW:(half + 1) * WINDOW]
        return weight

    def row_pass(weight, slot):
        image = lax.dot_general(
            passed[slot], row_mat[slot], NT, preferred_element_type=jnp.float32)
        power = image * image
        total = power[:BLOCK]
        for comp in range(1, comps):
            total = total + power[comp * BLOCK:(comp + 1) * BLOCK]
        return weight * total

    def sources_from(first, count):
        total = jnp.zeros((BLOCK, WINDOW), jnp.float32)
        weights = []
        for turn in range(count + 1):
            if turn < count:
                weights.append(column_pass(lax.rem(me + first + turn, n_src), turn))
            if turn > 0:
                total = total + row_pass(weights[turn - 1], turn - 1)
        acc[:BLOCK, :] += total

    def later_sources(step, carry):
        sources_from(HEAD + step * TURNS, TURNS)
        return carry

    lax.fori_loop(1, HEAD, wait_taps, 0)
    sources_from(0, HEAD)
    lax.fori_loop(HEAD, n_src, wait_taps, 0)
    rounds, rest = divmod(n_src - HEAD, TURNS)
    lax.fori_loop(0, rounds, later_sources, 0)
    if rest > 0:
        sources_from(HEAD + rounds * TURNS, rest)

    turned = acc[...].T
    block_image = turned[:BLOCK] + turned[BLOCK:]
    for owner in range(per_group):
        mine[owner] = block_image[owner * local_rows:(owner + 1) * local_rows]

    my_place = lax.rem(me, per_group)

    def out_copy(step):
        owner = lax.rem(my_place + step, per_group)
        return pltpu.make_async_remote_copy(
            src_ref=mine.at[owner], dst_ref=gathered.at[my_col],
            send_sem=o_send.at[step], recv_sem=o_recv.at[my_col],
            device_id={"src": my_row * per_group + owner}, device_id_type=MESH)

    def send_out(step, carry):
        out_copy(step).start()
        return carry

    lax.fori_loop(1, per_group, send_out, 0)
    gathered[my_col] = mine[my_place]

    def wait_out(step, carry):
        col = lax.rem(my_col + step, col_blocks)
        pltpu.make_async_remote_copy(
            src_ref=gathered.at[col], dst_ref=gathered.at[col],
            send_sem=o_send.at[0], recv_sem=o_recv.at[col],
            device_id={"src": me}, device_id_type=MESH).wait_recv()
        return carry

    lax.fori_loop(1, col_blocks, wait_out, 0)
    for pair in range(col_blocks // 2):
        out_ref[0, :, pair * WINDOW:(pair + 1) * WINDOW] = gathered[2 * pair] + pltpu.roll(
            gathered[2 * pair + 1], BLOCK, 1)

    def drain(step, carry):
        col = lax.rem(my_col + step, col_blocks)

        @pl.when(jnp.logical_not(is_self(col)))
        def _():
            field_copy(col, own_group, first_slot, step).wait_send()

        @pl.when(second_ok)
        def _():
            field_copy(col, second, second_slot, col_blocks + step).wait_send()

        return carry

    lax.fori_loop(0, col_blocks, drain, 0)

    def drain_taps(step, carry):
        taps_copy(step).wait_send()
        return carry

    lax.fori_loop(1, n_src, drain_taps, 0)

    def drain_out(step, carry):
        out_copy(step).wait_send()
        return carry

    lax.fori_loop(1, per_group, drain_out, 0)


def per_device(near_field, x_taps, y_taps, source_weight):
    n_src = lax.axis_size("src")
    n_tile = lax.axis_size("tile")
    _, local_rows, _, comps, width = near_field.shape
    _, _, ranks, tap_count = x_taps.shape
    rim = (tap_count - 1) // 2
    col_blocks = width // BLOCK
    per_group = BLOCK // local_rows
    assert WINDOW == BLOCK + 2 * rim and x_taps.shape[0] == 1
    assert n_src == col_blocks * (n_src * local_rows // BLOCK) and per_group == col_blocks

    rows_last = near_field[0].transpose(0, 2, 1, 3).reshape(comps * local_rows, 2, width)
    slots = WINDOW // local_rows
    dma = pltpu.SemaphoreType.DMA
    bf16, f32 = jnp.bfloat16, jnp.float32
    vmem = pl.BlockSpec(memory_space=pltpu.VMEM)
    anywhere = pl.BlockSpec(memory_space=pl.ANY)
    dims = (n_src, n_tile, local_rows, comps, ranks, tap_count)
    return pl.pallas_call(
        functools.partial(kernel, dims),
        out_shape=pltpu.VMEM((1, local_rows, width), f32),
        in_specs=[anywhere] * 4,
        out_specs=vmem,
        scratch_shapes=[
            pltpu.VMEM((comps * local_rows, 2, width), bf16),
            pltpu.VMEM((2, ranks, tap_count), bf16),
            pltpu.VMEM((2, ranks, tap_count), bf16),
            pltpu.VMEM((1, 1), f32),
            pltpu.VMEM((2 * comps * local_rows, width + WINDOW), f32),
            pltpu.VMEM((col_blocks, 2 * comps * local_rows, WINDOW), bf16),
            pltpu.VMEM((4 * ranks, WINDOW), bf16),
            pltpu.VMEM((slots, 2 * comps * local_rows, WINDOW), bf16),
            pltpu.VMEM((n_src, 4 * ranks, WINDOW), bf16),
            pltpu.VMEM((2 * comps * WINDOW, WINDOW), f32),
            pltpu.VMEM((2 * comps * WINDOW, 2 * WINDOW), bf16),
            pltpu.VMEM((TURNS, ranks * BLOCK, 2 * WINDOW), bf16),
            pltpu.VMEM((TURNS, 2 * BLOCK, 2 * ranks * WINDOW), bf16),
            pltpu.VMEM((TURNS, comps * BLOCK, 2 * ranks * WINDOW), bf16),
            pltpu.VMEM((WINDOW, WINDOW), f32),
            pltpu.VMEM((per_group, local_rows, WINDOW), f32),
            pltpu.VMEM((col_blocks, local_rows, WINDOW), f32),
            dma((4,)),
            dma((2 * col_blocks,)),
            dma((slots,)),
            dma((n_src,)),
            dma((n_src,)),
            dma((per_group,)),
            dma((col_blocks,)),
        ],
        compiler_params=pltpu.CompilerParams(collective_id=0, has_side_effects=True),
    )(rows_last, x_taps[0], y_taps[0], source_weight.reshape(1, 1))


def solution(mesh):
    placed = (
        P(("group", "tile"), "src", None, None, None),
        P("src", None, None, None),
        P("src", None, None, None),
        P("src"),
    )
    return jax.shard_map(
        per_device,
        mesh=mesh,
        in_specs=placed,
        out_specs=P(("group", "tile"), "src", None),
        check_vma=False,
    )
```
